768 devices in a mesh: dp: 32 (over z_hi, y), tensor: 24 (over x, z_lo, core).
Axes of the slice: x: 4, y: 8, z: 12 (z_hi: 4, z_lo: 3; z = z_hi * 3 + z_lo), core: 2. Of those that a mesh axis runs over, the one named last changes fastest.
Arguments:
- activations: bfloat16 [30720, 29568], P('dp', 'tensor'), may hold values from -6 to 6
- out_grad: bfloat16 [30720, 8192], P(('dp', 'tensor')), may hold values from -6 to 6
- projector: bfloat16 [8192, 512], replicated, may hold values from -0.0625 to 0.0625
- moment_one: float32 [512, 29568], P('dp', 'tensor'), may hold values from -3.01 to 3.01
- moment_two: float32 [512, 29568], P('dp', 'tensor'), may hold values from 0.001 to 1.001
Outputs:
- weight_step: bfloat16 [29568, 8192], P('tensor', 'dp')
- new_moment_one: float32 [512, 29568], P('dp', 'tensor')
- new_moment_two: float32 [512, 29568], P('dp', 'tensor')
The draws below stay inside these ranges and needn't reach their ends.
All inputs are finite; a program needn't handle non-finite values.
Results may differ from the reference program's by a relative error of at most 0.0056.
Values may be sent and summed in bfloat16 or wider, within the bound.
A program may use at most 32 MiB of HBM per device.

```python
import math
import jax
import jax.numpy as jnp

D = 8192
FF = 29568
R = 512
TOKENS = 30720


def second_moment(key):
    uniform_draw = jax.random.uniform(jax.random.fold_in(key, 17), (R, FF), jnp.float32)
    return 0.001 * jnp.exp(math.log(1000.0) * uniform_draw)


def draw_moment_two(key, part):
    return second_moment(key)


def draw_moment_one(key, part):
    scale_root = jnp.sqrt(second_moment(key))
    factor = jax.random.truncated_normal(jax.random.fold_in(key, 29), -3.0, 3.0, (R, FF), jnp.float32)
    return scale_root * factor


def levels(rng, extent, pieces, smallest, top_value):
    def one(position, shards_of):
        steps = jax.random.uniform(jax.random.fold_in(jax.random.fold_in(rng, 6), position), (shards_of,), jnp.float32, smallest / len(pieces), top_value / len(pieces))
        return jnp.repeat(jnp.exp(steps), extent[position] // shards_of).reshape((-1,) + (1,) * (len(extent) - position - 1))

    loudness = one(*pieces[0])
    for cut in pieces[1:]:
        loudness = loudness * one(*cut)
    return loudness


def normal_values(own_key, dims, width, most, cuts=(), dtype=jnp.bfloat16):
    entries = jax.random.normal(own_key, dims, jnp.float32) * width
    if len(cuts) > 0:
        entries = levels(own_key, dims, cuts, -0.22, 0.18) * entries
    return jnp.clip(entries, min=-most, max=most).astype(dtype)


def setup_inputs(seed: int = 0) -> dict:
    splits = jax.random.split(jax.random.key(seed), 6)
    return {
        "activations": normal_values(splits[0], (TOKENS, FF), 1.0, 6.0, ((0, 32), (1, 24))),
        "out_grad": normal_values(splits[1], (TOKENS, D), 1.0, 6.0, ((0, 768),)),
        "projector": normal_values(splits[2], (D, R), D ** -0.5, 0.0625),
        "moment_one": draw_moment_one(jax.random.fold_in(splits[5], 71), 0),
        "moment_two": draw_moment_two(jax.random.fold_in(splits[5], 71), 0),
    }


beta_one = 0.9
beta_two = 0.999
epsilon = 1e-08
bias_one = 1.0 - math.exp(1000.0 * math.log(0.9))
bias_two = 1.0 - math.exp(1000.0 * math.log(0.999))

def reference(activations, out_grad, projector, moment_one, moment_two):
    projected = jnp.dot(out_grad, projector, preferred_element_type=jnp.float32).astype(jnp.bfloat16)
    gradient = jnp.dot(projected.T, activations, preferred_element_type=jnp.float32)
    gradient = gradient * (1.0 / math.sqrt(TOKENS))
    new_one = beta_one * moment_one + (1.0 - beta_one) * gradient
    new_two = beta_two * moment_two + (1.0 - beta_two) * gradient * gradient
    update = (new_one / bias_one / (jnp.sqrt(new_two / bias_two) + epsilon)).astype(jnp.bfloat16)
    weight_step = jnp.dot(update.T, projector.T, preferred_element_type=jnp.float32).astype(jnp.bfloat16)
    return (weight_step, new_one, new_two)
```

```python
import functools
import math

import jax
import jax.numpy as jnp
from jax import lax
from jax.experimental import pallas as pl
from jax.experimental.pallas import tpu as pltpu
from jax.sharding import PartitionSpec as P

beta_one = 0.9
beta_two = 0.999
epsilon = 1e-08
bias_one = 1.0 - math.exp(1000.0 * math.log(0.9))
bias_two = 1.0 - math.exp(1000.0 * math.log(0.999))

NY, NZ = 8, 4
NX, NL, NC = 4, 3, 2
NT = NX * NL * NC
ND = NY * NZ
ROWS = 40
RANK = 512
OWN = RANK // ND
TOK = ROWS * NT
COLS = 1232
WIDE = 1280
DM = 8192
OUT = DM // ND
KC = 1024
SCALE = 1.0 / math.sqrt(ROWS * NT * ND)

RS_ORDER = (2, 1, 3, 0)
AG_ORDER = (0, 1, 3, 2)
RIGHT_HOPS = {2: 4, 1: 3, 3: 4, 0: 3}


def hops(o, way):
    return RIGHT_HOPS[o] if way == 0 else 7 - RIGHT_HOPS[o]


def kernel(
    act_hbm, og_hbm, proj_hbm, m1_hbm, m2_hbm,
    w_hbm, n1_hbm, n2_hbm,
    og, proj, act, pslice, m1, m2, n1, n2, wout,
    blocks, tokens, grad, sums_out, sums_in, z_out, z_in, upd,
    local_sem, out_sem, a_send, a_recv, rs_send, rs_recv, zs_send, zs_recv, ag_send, ag_recv,
):
    dp = lax.axis_index("dp")
    t = lax.axis_index("tensor")
    y, z = lax.rem(dp, NY), lax.div(dp, NY)
    core = lax.rem(t, NC)
    zl = lax.rem(lax.div(t, NC), NL)
    x = lax.div(t, NC * NL)

    def tensor_at(dx, dl, dc):
        xx = lax.rem(x + dx + NX, NX)
        ll = lax.rem(zl + dl, NL)
        cc = lax.rem(core + dc, NC)
        return (xx * NL + ll) * NC + cc

    def y_at(d):
        return lax.rem(y + d + NY, NY)

    def z_at(o):
        return lax.rem(z + o, NZ)

    def dev(dp_id=None, t_id=None):
        return {"dp": dp if dp_id is None else dp_id, "tensor": t if t_id is None else t_id}

    loads = [pltpu.make_async_copy(og_hbm, og, local_sem.at[0])]
    nk = DM // KC
    for k in range(nk):
        part = pl.ds(k * KC, KC)
        loads.append(pltpu.make_async_copy(proj_hbm.at[part], proj.at[part], local_sem.at[1 + k]))
    mine = pl.ds(pl.multiple_of(dp * OUT, OUT), OUT)
    late = [
        pltpu.make_async_copy(act_hbm, act, local_sem.at[nk + 1]),
        pltpu.make_async_copy(m1_hbm, m1, local_sem.at[nk + 2]),
        pltpu.make_async_copy(m2_hbm, m2, local_sem.at[nk + 3]),
        pltpu.make_async_copy(proj_hbm.at[mine], pslice, local_sem.at[nk + 4]),
    ]
    for copy in loads + late:
        copy.start()

    barrier = pltpu.get_barrier_semaphore()
    peers = [
        dev(t_id=tensor_at(0, 0, 1)),
        dev(t_id=tensor_at(1, 0, 0)), dev(t_id=tensor_at(-1, 0, 0)),
        dev(t_id=tensor_at(0, 1, 0)), dev(t_id=tensor_at(0, 2, 0)),
        dev(dp_id=z * NY + y_at(1)), dev(dp_id=z * NY + y_at(-1)),
    ] + [dev(dp_id=z_at(o) * NY + y) for o in (1, 2, 3)]
    for peer in peers:
        pl.semaphore_signal(barrier, inc=1, device_id=peer, device_id_type=pl.DeviceIdType.MESH)

    loads[0].wait()
    acc = jnp.zeros((ROWS, RANK), jnp.float32)
    for k in range(nk):
        loads[1 + k].wait()
        acc = acc + jnp.dot(
            og[:, k * KC:(k + 1) * KC], proj[k * KC:(k + 1) * KC, :],
            preferred_element_type=jnp.float32,
        )
    blocks[t] = acc.astype(jnp.bfloat16)
    grad[:, :, WIDE - 128:] = jnp.zeros((ND, OWN, 128), jnp.float32)
    pl.semaphore_wait(barrier, len(peers))

    sent = []

    def remote(src, dst, ssem, rsem, peer):
        return pltpu.make_async_remote_copy(
            src_ref=src, dst_ref=dst, send_sem=ssem, recv_sem=rsem,
            device_id=peer, device_id_type=pl.DeviceIdType.MESH,
        )

    def send(src, dst, ssem, rsem, peer):
        copy = remote(src, dst, ssem, rsem, peer)
        copy.start()
        sent.append(copy)

    count_a = [0]
    other = dev(t_id=tensor_at(0, 0, 1))

    def send_a(slot, peer):
        n = count_a[0]
        count_a[0] += 1
        send(blocks.at[slot], blocks.at[slot], a_send.at[n], a_recv.at[slot], peer)

    def wait_a(slot):
        remote(blocks.at[slot], blocks.at[slot], a_send.at[0], a_recv.at[slot], other).wait_recv()

    east, west = dev(t_id=tensor_at(1, 0, 0)), dev(t_id=tensor_at(-1, 0, 0))
    send_a(t, east)
    send_a(t, west)
    for dl in (1, 2):
        send_a(t, dev(t_id=tensor_at(0, dl, 0)))
    send_a(t, other)
    for dl in (1, 2):
        slot = tensor_at(0, dl, 0)
        wait_a(slot)
        send_a(slot, east)
        send_a(slot, west)
        send_a(slot, other)
    for dl in range(NL):
        way = 1 - 2 * lax.rem(core + dl, 2)
        near, far = tensor_at(-way, dl, 0), tensor_at(way, dl, 0)
        wait_a(near)
        send_a(near, dev(t_id=tensor_at(way, 0, 0)))
        send_a(near, other)
        wait_a(far)
        send_a(far, other)
    for dl in range(NL):
        slot = tensor_at(2, dl, 0)
        wait_a(slot)
        send_a(slot, other)
    for dx in (0, 1, -1, 2):
        for dl in range(NL):
            wait_a(tensor_at(dx, dl, 1))
    for pair in range(NT // 2):
        both = jnp.concatenate(
            [blocks[2 * pair].astype(jnp.float32), blocks[2 * pair + 1].astype(jnp.float32)], axis=0
        )
        tokens[pair * 2 * ROWS:(pair + 1) * 2 * ROWS, :] = both.astype(jnp.bfloat16)
    late[0].wait()

    ring = (dev(dp_id=z * NY + y_at(1)), dev(dp_id=z * NY + y_at(-1)))
    index = {}
    for o in RS_ORDER:
        for way in (0, 1):
            for s in range(hops(o, way)):
                index[o, way, s] = len(index)

    def push(o, way, s):
        n = index[o, way, s]
        sign = 1 if way == 0 else -1
        row = z_at(o) * NY + y_at(sign * (hops(o, way) - s))
        value = grad[row]
        if s > 0:
            value = value + sums_in[index[o, way, s - 1]].astype(jnp.float32)
        sums_out[n] = value.astype(jnp.bfloat16)
        send(sums_out.at[n], sums_in.at[n], rs_send.at[n], rs_recv.at[n], ring[way])

    def wait_rs(o, way, s):
        n = index[o, way, s]
        remote(sums_out.at[n], sums_in.at[n], rs_send.at[n], rs_recv.at[n], ring[1 - way]).wait_recv()

    for o in RS_ORDER:
        first = pl.multiple_of(z_at(o) * 128, 128)
        tile = lax.dot_general(
            tokens[:, pl.ds(first, 128)], act[...], (((0,), (0,)), ((), ())),
            preferred_element_type=jnp.float32,
        )
        grad[pl.ds(z_at(o) * NY, NY), :, :COLS] = tile.reshape(NY, OWN, COLS)
        for way in (0, 1):
            push(o, way, 0)

    events = []
    for place, o in enumerate(RS_ORDER):
        for way in (0, 1):
            for s in range(hops(o, way)):
                events.append((place * 1.7 + s * 2.5, place, s, way, o))
    left = {o: 2 for o in RS_ORDER}
    total = None
    for _, _, s, way, o in sorted(events):
        wait_rs(o, way, s)
        if s + 1 < hops(o, way):
            push(o, way, s + 1)
            continue
        left[o] -= 1
        if left[o]:
            continue
        value = grad[z_at(o) * NY + y]
        for w in (0, 1):
            value = value + sums_in[index[o, w, hops(o, w) - 1]].astype(jnp.float32)
        if o == 0:
            total = value
        else:
            z_out[o - 1] = value.astype(jnp.bfloat16)
            send(
                z_out.at[o - 1], z_in.at[o - 1], zs_send.at[o - 1], zs_recv.at[o - 1],
                dev(dp_id=z_at(o) * NY + y),
            )

    for o in (1, 3, 2):
        remote(z_out.at[o - 1], z_in.at[o - 1], zs_send.at[o - 1], zs_recv.at[o - 1], ring[0]).wait_recv()
        total = total + z_in[o - 1].astype(jnp.float32)

    for copy in late[1:]:
        copy.wait()
    gradient = total[:, :COLS] * SCALE
    new_one = beta_one * m1[...] + (1.0 - beta_one) * gradient
    new_two = beta_two * m2[...] + (1.0 - beta_two) * gradient * gradient
    update = new_one / bias_one / (jnp.sqrt(new_two / bias_two) + epsilon)
    own = z * NY + y
    upd[own, :, WIDE - 128:] = jnp.zeros((OWN, 128), jnp.bfloat16)
    upd[own, :, :COLS] = update.astype(jnp.bfloat16)
    n1[...] = new_one
    n2[...] = new_two

    count_g = [0]

    def send_g(slot, peer):
        n = count_g[0]
        count_g[0] += 1
        send(upd.at[slot], upd.at[slot], ag_send.at[n], ag_recv.at[slot], peer)

    def wait_g(slot):
        remote(upd.at[slot], upd.at[slot], ag_send.at[0], ag_recv.at[slot], other).wait_recv()

    send_g(own, ring[0])
    send_g(own, ring[1])
    for o in (2, 1, 3):
        send_g(own, dev(dp_id=z_at(o) * NY + y))
    outs = [
        pltpu.make_async_copy(n1, n1_hbm, out_sem.at[0]),
        pltpu.make_async_copy(n2, n2_hbm, out_sem.at[1]),
    ]
    for copy in outs:
        copy.start()

    arrives = {0: 0.0, 1: 3.6, 3: 3.8, 2: 5.8}
    events = []
    for o in AG_ORDER:
        if o:
            events.append((arrives[o], 0, o, 0, -1))
        for way in (0, 1):
            for s in range(hops(o, way)):
                events.append((arrives[o] + 2.3 * (s + 1), 1, o, way, s))
    for _, _, o, way, s in sorted(events):
        base = z_at(o) * NY
        if s < 0:
            wait_g(base + y)
            send_g(base + y, ring[0])
            send_g(base + y, ring[1])
            continue
        slot = base + y_at(-(s + 1) if way == 0 else s + 1)
        wait_g(slot)
        if s + 1 < hops(o, way):
            send_g(slot, ring[way])

    for m in range(0, COLS, 256):
        width = min(256, WIDE - m)
        part = upd[:, :, m:m + width].reshape(RANK, width)
        tile = lax.dot_general(
            part, pslice[...], (((0,), (1,)), ((), ())), preferred_element_type=jnp.float32
        )
        rows = min(width, COLS - m)
        wout[m:m + rows, :] = tile[:rows].astype(jnp.bfloat16)
    outs.append(pltpu.make_async_copy(wout, w_hbm, out_sem.at[2]))
    outs[-1].start()
    for copy in sent:
        copy.wait_send()
    for copy in outs:
        copy.wait()


def per_device(activations, out_grad, projector, moment_one, moment_two):
    bf16, f32 = jnp.bfloat16, jnp.float32
    dma = pltpu.SemaphoreType.DMA
    return pl.pallas_call(
        kernel,
        out_shape=(
            jax.ShapeDtypeStruct((COLS, OUT), bf16),
            jax.ShapeDtypeStruct((OWN, COLS), f32),
            jax.ShapeDtypeStruct((OWN, COLS), f32),
        ),
        in_specs=[pl.BlockSpec(memory_space=pl.ANY)] * 5,
        out_specs=[pl.BlockSpec(memory_space=pl.ANY)] * 3,
        scratch_shapes=[
            pltpu.VMEM((ROWS, DM), bf16),
            pltpu.VMEM((DM, RANK), bf16),
            pltpu.VMEM((TOK, COLS), bf16),
            pltpu.VMEM((OUT, RANK), bf16),
            pltpu.VMEM((OWN, COLS), f32),
            pltpu.VMEM((OWN, COLS), f32),
            pltpu.VMEM((OWN, COLS), f32),
            pltpu.VMEM((OWN, COLS), f32),
            pltpu.VMEM((COLS, OUT), bf16),
            pltpu.VMEM((NT, ROWS, RANK), bf16),
            pltpu.VMEM((TOK, RANK), bf16),
            pltpu.VMEM((ND, OWN, WIDE), f32),
            pltpu.VMEM((28, OWN, WIDE), bf16),
            pltpu.VMEM((28, OWN, WIDE), bf16),
            pltpu.VMEM((3, OWN, WIDE), bf16),
            pltpu.VMEM((3, OWN, WIDE), bf16),
            pltpu.VMEM((ND, OWN, WIDE), bf16),
            dma((DM // KC + 5,)),
            dma((3,)),
            dma((23,)),
            dma((NT,)),
            dma((28,)),
            dma((28,)),
            dma((3,)),
            dma((3,)),
            dma((31,)),
            dma((ND,)),
        ],
        compiler_params=pltpu.CompilerParams(
            collective_id=0, has_side_effects=True, vmem_limit_bytes=50 * 2**20
        ),
        name="galore_step",
    )(activations, out_grad, projector, moment_one, moment_two)


def solution(mesh):
    placed = (
        P("dp", "tensor"),
        P(("dp", "tensor"), None),
        P(),
        P("dp", "tensor"),
        P("dp", "tensor"),
    )
    return jax.shard_map(
        per_device,
        mesh=mesh,
        in_specs=placed,
        out_specs=(P("tensor", "dp"), P("dp", "tensor"), P("dp", "tensor")),
        check_vma=False,
    )
```
